32 devices in a mesh: group: 2 (over x), sample: 16 (over z, y, core).
Axes of the slice: x: 2, y: 2, z: 4, core: 2. Of those that a mesh axis runs over, the one named last changes fastest.
Arguments:
- queries: bfloat16 [32, 3, 64, 128], P(('group', 'sample')), parts along dimension 0, may hold values from -150 to 150
- prefix_keys: bfloat16 [4096, 8, 128], P(('group', 'sample')), parts along dimension 0, may hold values from -5 to 5
- prefix_values: bfloat16 [4096, 8, 128], P(('group', 'sample')), parts along dimension 0, may hold values from -6 to 6
- suffix_keys: bfloat16 [32, 1024, 8, 128], P(('group', 'sample')), parts along dimension 0, may hold values from -7 to 7
- suffix_values: bfloat16 [32, 1024, 8, 128], P(('group', 'sample')), parts along dimension 0, may hold values from -6 to 6
- suffix_lengths: int32 [32], P(('group', 'sample')), parts along dimension 0, may hold values from 0 to 1024, as said below
- new_keys: bfloat16 [32, 3, 8, 128], P(('group', 'sample')), parts along dimension 0, may hold values from -5 to 5
- new_values: bfloat16 [32, 3, 8, 128], P(('group', 'sample')), parts along dimension 0, may hold values from -6 to 6
Outputs:
- attention: float32 [32, 3, 64, 128], P(('group', 'sample')), parts along dimension 0
The draws below stay inside these ranges and needn't reach their ends.
There are 2 independent parts, one for each index of `group`. The reference program is written for one: setup_inputs(seed, part) draws one part's arguments, and reference() takes and returns one part's arrays. A program takes and returns all parts, laid end to end along the dimension named above; each array names one. Nothing has to cross between parts.
Inputs may be any that keep to these rules, and one draw needn't show every extreme that they name: `suffix_lengths`: some sample of every group has exactly 1024 generated tokens.
All inputs are finite; a program needn't handle non-finite values.
Results may differ from the reference program's by a relative error of at most 0.00042.
Values may be sent and summed in bfloat16 or wider, within the bound.
A program may use at most 128 MiB of HBM per device.

```python
import jax
import jax.numpy as jnp
from jax import lax

H = 64
KVH = 8
HD = 128
STEPS = 3
PRE_DEV = 128
SUF = 1024
SAMPLES = 16
PREFIX = 2048
N_SAMPLE = 16


def shared_draw(key):
    prompt_keys = jax.random.truncated_normal(jax.random.fold_in(key, 11), -5.0, 5.0, (PREFIX, KVH, HD), jnp.float32)
    fresh_keys = jax.random.truncated_normal(jax.random.fold_in(key, 12), -5.0, 5.0, (SAMPLES, STEPS, KVH, HD), jnp.float32)
    noise = 3.0 * jax.random.normal(jax.random.fold_in(key, 13), (SAMPLES, STEPS, H, HD), jnp.float32)
    query_draw = noise + 1.4 * jnp.repeat(fresh_keys, H // KVH, axis=2)
    query_draw = jnp.clip(query_draw, -150.0, 150.0)
    return (prompt_keys, fresh_keys, query_draw)


def draw_queries(key, part):
    return shared_draw(key)[2].astype(jnp.bfloat16)


def draw_prefix_keys(key, part):
    return shared_draw(key)[0].astype(jnp.bfloat16)


def draw_new_keys(key, part):
    return shared_draw(key)[1].astype(jnp.bfloat16)


def draw_suffix_lengths(key, part):
    first_draw = jax.random.randint(jax.random.fold_in(key, 21), (SAMPLES,), 0, SUF + 1, jnp.int32)
    second_draw = jax.random.randint(jax.random.fold_in(key, 22), (SAMPLES,), 0, SUF + 1, jnp.int32)
    lengths = first_draw * second_draw // SUF
    chosen = jax.random.randint(jax.random.fold_in(key, 23), (), 0, SAMPLES, jnp.int32)
    return jnp.where(jnp.arange(SAMPLES, dtype=jnp.int32) == chosen, SUF, lengths).astype(jnp.int32)


def level_of(stream_key, dims, cuts, least, top_value):
    def one(position, shards_of):
        draws = jax.random.uniform(jax.random.fold_in(jax.random.fold_in(stream_key, 6), position), (shards_of,), jnp.float32, least / len(cuts), top_value / len(cuts))
        return jnp.repeat(jnp.exp(draws), dims[position] // shards_of).reshape((-1,) + (1,) * (len(dims) - position - 1))

    loudness = one(*cuts[0])
    for cut in cuts[1:]:
        loudness = loudness * one(*cut)
    return loudness


def normal_values(stream_key, shape, spread, reach, shards=(), held_as=jnp.bfloat16):
    result = spread * jax.random.normal(stream_key, shape, jnp.float32)
    if shards:
        result = result * level_of(stream_key, shape, shards, -0.22, 0.18)
    return jnp.clip(result, -reach, reach).astype(held_as)


def setup_inputs(seed: int = 0, part: int = 0) -> dict:
    key_of = jax.random.split(jax.random.key(seed), 9)
    part_keys = jax.random.split(jax.random.fold_in(key_of[8], part), 9)
    queries = draw_queries(jax.random.fold_in(jax.random.fold_in(key_of[8], part), 71), part)
    prefix_keys = draw_prefix_keys(jax.random.fold_in(jax.random.fold_in(key_of[8], part), 71), part)
    prefix_values = normal_values(part_keys[2], (PREFIX, KVH, HD), 1.0, 6.0, ((0, 16),))
    suffix_keys = normal_values(part_keys[3], (SAMPLES, SUF, KVH, HD), 1.2, 7.0, ((0, 16),))
    suffix_values = normal_values(part_keys[4], (SAMPLES, SUF, KVH, HD), 1.0, 6.0, ((0, 16),))
    suffix_lengths = draw_suffix_lengths(jax.random.fold_in(jax.random.fold_in(key_of[8], part), 71), part)
    new_keys = draw_new_keys(jax.random.fold_in(jax.random.fold_in(key_of[8], part), 71), part)
    new_values = normal_values(part_keys[7], (SAMPLES, STEPS, KVH, HD), 1.0, 6.0, ((0, 16),))
    return dict(queries=queries, prefix_keys=prefix_keys, prefix_values=prefix_values, suffix_keys=suffix_keys, suffix_values=suffix_values, suffix_lengths=suffix_lengths, new_keys=new_keys, new_values=new_values)


def reference(queries, prefix_keys, prefix_values, suffix_keys, suffix_values, suffix_lengths, new_keys, new_values):
    group_size = H // KVH
    factor = 1.0 / jnp.sqrt(jnp.float32(HD))
    piece_keys = prefix_keys.astype(jnp.float32).reshape(N_SAMPLE, PRE_DEV, KVH, HD)
    piece_values = prefix_values.astype(jnp.float32).reshape(N_SAMPLE, PRE_DEV, KVH, HD)
    step_index = jnp.arange(STEPS, dtype=jnp.int32)
    causal = step_index[None, :] <= step_index[:, None]
    positions = jnp.arange(SUF, dtype=jnp.int32)

    def one_sample(sample_data):
        own_queries, own_keys, own_values, length, fresh_keys, fresh_values = sample_data
        query_rows = own_queries.astype(jnp.float32).reshape(STEPS, KVH, group_size, HD)
        scores = jnp.einsum('thgd,nphd->nthgp', query_rows, piece_keys, precision=lax.Precision.HIGHEST) * factor
        maxima = lax.optimization_barrier(jnp.max(scores, axis=-1))
        powers = jnp.exp(scores - maxima[..., None])
        totals = lax.optimization_barrier(jnp.sum(powers, axis=-1))
        sums = jnp.einsum('nthgp,nphd->nthgd', powers, piece_values, precision=lax.Precision.HIGHEST)
        pieces = sums / totals[..., None]
        log_totals = maxima + jnp.log(totals)
        all_keys = jnp.concatenate([own_keys, fresh_keys], axis=0).astype(jnp.float32)
        all_values = jnp.concatenate([own_values, fresh_values], axis=0).astype(jnp.float32)
        own_scores = jnp.einsum('thgd,phd->thgp', query_rows, all_keys, precision=lax.Precision.HIGHEST) * factor
        in_range = jnp.broadcast_to((positions < length)[None, :], (STEPS, SUF))
        usable = jnp.concatenate([in_range, causal], axis=1)[:, None, None, :]
        own_scores = jnp.where(usable, own_scores, -jnp.inf)
        own_max = lax.optimization_barrier(jnp.max(own_scores, axis=-1))
        own_powers = jnp.where(usable, jnp.exp(own_scores - own_max[..., None]), 0.0)
        own_total = lax.optimization_barrier(jnp.sum(own_powers, axis=-1))
        own_rounded = lax.optimization_barrier(own_powers.astype(jnp.bfloat16)).astype(jnp.float32)
        own_sum = jnp.einsum('thgp,phd->thgd', own_rounded, all_values, precision=lax.Precision.HIGHEST)
        highest = jnp.maximum(lax.optimization_barrier(jnp.max(log_totals, axis=0)), own_max)
        weights = jnp.exp(log_totals - highest[None])
        own_weight = jnp.exp(own_max - highest)
        upper = lax.optimization_barrier(jnp.sum(weights[..., None] * pieces, axis=0)) + own_weight[..., None] * own_sum
        lower = lax.optimization_barrier(jnp.sum(weights, axis=0)) + own_weight * own_total
        return (upper / lower[..., None]).reshape(STEPS, H, HD)
    return lax.map(one_sample, (queries, suffix_keys, suffix_values, suffix_lengths, new_keys, new_values))
```

```python
import functools
import math

import jax
import jax.numpy as jnp
from jax import lax
from jax.experimental import pallas as pl
from jax.experimental.pallas import tpu as pltpu
from jax.sharding import PartitionSpec as P

F32, BF16 = jnp.float32, jnp.bfloat16


def rows_of(tiles):
    wide = tiles.astype(F32)
    return wide.reshape(math.prod(wide.shape[:-1]), wide.shape[-1])


def nt_dot(a, b):
    return lax.dot_general(a, b, (((1,), (1,)), ((), ())), preferred_element_type=F32)


def kernel(
    n, group, chunk,
    len_ref, q_hbm, pk_hbm, pv_hbm, sk_hbm, sv_hbm, nk_hbm, nv_hbm,
    out_ref,
    q_own, pk, pv, wide, k_send, v_send, q_all, k_all, v_all, sk, sv, nk, nv, s_own,
    o_send, l_send, o_all, l_all,
    local_sem, suf_sem, q_ss, q_rs, k_ss, k_rs, v_ss, v_rs, o_ss, o_rs, l_ss, l_rs,
):
    steps, kvh, gsize, dim = q_hbm.shape
    per = steps * gsize
    tokens = pk.shape[0] // kvh
    factor = 1.0 / math.sqrt(dim)
    me = lax.axis_index("sample")
    head = lax.rem(me, kvh)
    base = me - head
    chunks = sk.shape[0] // chunk

    def remote(src, dst, ss, rs, dev):
        return pltpu.make_async_remote_copy(
            src_ref=src, dst_ref=dst, send_sem=ss, recv_sem=rs,
            device_id={"sample": dev}, device_id_type=pl.DeviceIdType.MESH,
        )

    local = [
        pltpu.make_async_copy(a, b, local_sem.at[i])
        for i, (a, b) in enumerate(
            [(pk_hbm, pk), (pv_hbm, pv), (q_hbm, q_own), (nk_hbm, nk), (nv_hbm, nv)]
        )
    ]
    for c in local:
        c.start()
    own_q = pltpu.make_async_copy(q_hbm.at[:, head], q_all.at[me], q_rs.at[me])
    own_q.start()
    halves = []
    for i, (a, b) in enumerate([(sk_hbm, sk), (sv_hbm, sv)]):
        for c in range(chunks):
            part = pl.ds(c * chunk, chunk)
            halves.append(
                pltpu.make_async_copy(a.at[part], b.at[part], suf_sem.at[i * chunks + c])
            )
    for c in halves:
        c.start()

    barrier = pltpu.get_barrier_semaphore()

    def greet(d, _):
        pl.semaphore_signal(
            barrier, inc=1, device_id={"sample": lax.rem(me + d, n)},
            device_id_type=pl.DeviceIdType.MESH,
        )
        return 0

    lax.fori_loop(1, n, greet, 0)

    for src, copy, dst, mine in ((pk, local[0], k_send, k_all), (pv, local[1], v_send, v_all)):
        copy.wait()
        wide[...] = src[...].astype(F32)
        for h in range(kvh):
            dst[h] = wide[pl.ds(h, tokens, stride=kvh), :].astype(BF16)
        mine[head] = wide[pl.ds(head, tokens, stride=kvh), :].astype(BF16)

    pl.semaphore_wait(barrier, n - 1)

    def q_copy(d):
        dev = lax.rem(me + d, n)
        return remote(q_hbm.at[:, lax.rem(dev, kvh)], q_all.at[me], q_ss.at[d], q_rs.at[me], dev)

    def kv_copy(d, src, dst, ss, rs):
        hd = lax.rem(head + d, kvh)
        return remote(src.at[hd], dst.at[head], ss.at[d], rs.at[head], base + hd)

    def start(copy):
        def body(d, _):
            copy(d).start()
            return 0
        return body

    k_copy = lambda d: kv_copy(d, k_send, k_all, k_ss, k_rs)
    v_copy = lambda d: kv_copy(d, v_send, v_all, v_ss, v_rs)
    lax.fori_loop(1, n, start(q_copy), 0)
    lax.fori_loop(1, kvh, start(k_copy), 0)
    lax.fori_loop(1, kvh, start(v_copy), 0)

    for c in local[2:]:
        c.wait()
    rows = kvh * per
    q_rows = jnp.concatenate(
        [q_own[t, h].astype(F32) for h in range(kvh) for t in range(steps)], axis=0
    ).astype(BF16)
    length = len_ref[0]
    row = lax.broadcasted_iota(jnp.int32, (rows, 128), 0)
    lane = lax.broadcasted_iota(jnp.int32, (rows, 128), 1)
    lane_head = lax.rem(lane, kvh)
    match = (row >= lane_head * per) & (row < (lane_head + 1) * per)
    bias = jnp.where(match, 0.0, -jnp.inf).astype(F32)
    bias_wide = jnp.concatenate([bias] * (chunk // 128), axis=1)
    token_of = lax.div(lax.broadcasted_iota(jnp.int32, (8, chunk), 1), kvh)

    top = jnp.full((rows, 1), -jnp.inf, F32)
    for c in range(chunks):
        halves[c].wait()
        s = nt_dot(q_rows, sk[c * chunk:(c + 1) * chunk, :]) * factor
        limit = jnp.where(token_of < length - c * (chunk // kvh), 0.0, -jnp.inf).astype(F32)[:1]
        s = s + bias_wide + limit
        s_own[c] = s
        top = jnp.maximum(top, jnp.max(s, axis=-1, keepdims=True))

    pad = jnp.zeros((128 - steps * kvh, dim), F32)
    new_k = jnp.concatenate([nk[j].astype(F32) for j in range(steps)] + [pad], axis=0).astype(BF16)
    new_v = jnp.concatenate([nv[j].astype(F32) for j in range(steps)] + [pad], axis=0).astype(BF16)
    step_of = lax.div(lax.rem(row, per), gsize)
    s_new = nt_dot(q_rows, new_k) * factor + bias
    s_new = jnp.where(lax.div(lane, kvh) <= step_of, s_new, -jnp.inf)
    own_max = jnp.maximum(top, jnp.max(s_new, axis=-1, keepdims=True))
    w_new = jnp.exp(s_new - own_max)
    own_total = jnp.sum(w_new, axis=-1, keepdims=True)
    own_sum = jnp.dot(w_new.astype(BF16), new_v, preferred_element_type=F32)
    for c in range(chunks):
        halves[chunks + c].wait()
        w = jnp.exp(s_own[c] - own_max)
        own_total = own_total + jnp.sum(w, axis=-1, keepdims=True)
        own_sum = own_sum + jnp.dot(
            w.astype(BF16), sv[c * chunk:(c + 1) * chunk, :], preferred_element_type=F32
        )

    own_q.wait()

    def arrive(make, rs):
        def body(d, _):
            make(d, rs).wait_recv()
            return 0
        return body

    def q_in(d, _):
        src = lax.rem(me + d, n)
        return remote(q_hbm.at[:, head], q_all.at[src], q_ss.at[d], q_rs.at[src], src)

    def kv_in(src, dst, ss, rs):
        def make(d, _):
            hd = lax.rem(head + d, kvh)
            return remote(src.at[hd], dst.at[hd], ss.at[d], rs.at[hd], base + hd)
        return make

    lax.fori_loop(1, n, arrive(q_in, None), 0)
    lax.fori_loop(1, kvh, arrive(kv_in(k_send, k_all, k_ss, k_rs), None), 0)
    lax.fori_loop(1, kvh, arrive(kv_in(v_send, v_all, v_ss, v_rs), None), 0)

    diag_row = lax.broadcasted_iota(jnp.int32, (per, 128), 0)
    diag_lane = lax.broadcasted_iota(jnp.int32, (per, 128), 1)
    diag = diag_row == diag_lane

    def out_copy(dev):
        return remote(o_send.at[dev], o_all.at[me], o_ss.at[dev], o_rs.at[me], dev)

    def log_copy(dev):
        return remote(l_send.at[dev], l_all.at[me], l_ss.at[dev], l_rs.at[me], dev)

    keys = k_all[...].reshape(kvh * tokens, dim)
    values = v_all[...].reshape(kvh * tokens, dim)
    groups = n // group

    def block(i, _):
        first = lax.rem(lax.div(me, group) + 1 + i, groups) * group
        q_block = rows_of(q_all[pl.ds(first, group)]).astype(BF16)
        s = nt_dot(q_block, keys) * factor
        m = jnp.max(s, axis=-1, keepdims=True)
        w = jnp.exp(s - m)
        total = jnp.sum(w, axis=-1, keepdims=True)
        high = w.astype(BF16)
        low = (w - high.astype(F32)).astype(BF16)
        sums = jnp.dot(high, values, preferred_element_type=F32) + jnp.dot(
            low, values, preferred_element_type=F32
        )
        o_send[pl.ds(first, group)] = (sums / total).reshape(group, per, dim)
        logs = jnp.broadcast_to(m + jnp.log(total), (group * per, 128)).reshape(group, per, 128)
        l_send[pl.ds(first, group)] = jnp.sum(
            jnp.where(diag[None], logs, 0.0), axis=1, keepdims=True
        )
        for j in range(group):
            dev = first + j

            @pl.when(dev != me)
            def _():
                out_copy(dev).start()
                log_copy(dev).start()

        return 0

    lax.fori_loop(0, groups, block, 0)
    mine_o = pltpu.make_async_copy(o_send.at[me], o_all.at[me], o_rs.at[me])
    mine_l = pltpu.make_async_copy(l_send.at[me], l_all.at[me], l_rs.at[me])
    mine_o.start()
    mine_l.start()

    def drain(d, _):
        q_copy(d).wait_send()
        return 0

    def drain_kv(d, _):
        k_copy(d).wait_send()
        v_copy(d).wait_send()
        return 0

    lax.fori_loop(1, n, drain, 0)
    lax.fori_loop(1, kvh, drain_kv, 0)
    mine_o.wait()
    mine_l.wait()

    def results_in(d, _):
        src = lax.rem(me + d, n)
        remote(o_send.at[src], o_all.at[src], o_ss.at[src], o_rs.at[src], src).wait_recv()
        remote(l_send.at[src], l_all.at[src], l_ss.at[src], l_rs.at[src], src).wait_recv()
        return 0

    lax.fori_loop(1, n, results_in, 0)

    repeats = n // kvh
    logs = jnp.sum(
        jnp.where(diag[None], jnp.broadcast_to(l_all[...], (n, per, 128)), 0.0),
        axis=-1, keepdims=True,
    ).reshape(repeats, rows, 1)
    largest = jnp.maximum(jnp.max(logs, axis=0), own_max)
    weights = jnp.exp(logs - largest[None])
    share = jnp.exp(own_max - largest)
    upper = share * own_sum
    lower = share * own_total
    for r in range(repeats):
        piece = o_all[r * kvh:(r + 1) * kvh].reshape(rows, dim)
        upper = upper + weights[r] * piece
        lower = lower + weights[r]
    result = upper / lower
    for h in range(kvh):
        for t in range(steps):
            at = h * per + t * gsize
            out_ref[t, h] = result[at:at + gsize]

    def drain_out(d, _):
        dev = lax.rem(me + d, n)
        out_copy(dev).wait_send()
        log_copy(dev).wait_send()
        return 0

    lax.fori_loop(1, n, drain_out, 0)


def solution(mesh):
    n = mesh.shape["sample"]

    def shards(queries, pk, pv, sk, sv, lengths, nk, nv):
        _, steps, heads, dim = queries.shape
        tokens, kvh, _ = pk.shape
        gsize = heads // kvh
        suffix = sk.shape[1]
        per = steps * gsize
        group = math.gcd(n, 4)
        chunk = math.gcd(suffix * kvh, 1024)
        chunks = suffix * kvh // chunk
        any_spec = pl.BlockSpec(memory_space=pl.ANY)
        dma = pltpu.SemaphoreType.DMA
        out = pl.pallas_call(
            functools.partial(kernel, n, group, chunk),
            out_shape=jax.ShapeDtypeStruct((steps, kvh, gsize, dim), F32),
            in_specs=[pl.BlockSpec(memory_space=pltpu.SMEM)] + [any_spec] * 7,
            out_specs=pl.BlockSpec(memory_space=pltpu.VMEM),
            scratch_shapes=[
                pltpu.VMEM((steps, kvh, gsize, dim), BF16),
                pltpu.VMEM((tokens * kvh, dim), BF16),
                pltpu.VMEM((tokens * kvh, dim), BF16),
                pltpu.VMEM((tokens * kvh, dim), F32),
                pltpu.VMEM((kvh, tokens, dim), BF16),
                pltpu.VMEM((kvh, tokens, dim), BF16),
                pltpu.VMEM((n, steps, gsize, dim), BF16),
                pltpu.VMEM((kvh, tokens, dim), BF16),
                pltpu.VMEM((kvh, tokens, dim), BF16),
                pltpu.VMEM((suffix * kvh, dim), BF16),
                pltpu.VMEM((suffix * kvh, dim), BF16),
                pltpu.VMEM((steps, kvh, dim), BF16),
                pltpu.VMEM((steps, kvh, dim), BF16),
                pltpu.VMEM((chunks, kvh * per, chunk), F32),
                pltpu.VMEM((n, per, dim), F32),
                pltpu.VMEM((n, 1, 128), F32),
                pltpu.VMEM((n, per, dim), F32),
                pltpu.VMEM((n, 1, 128), F32),
                dma((5,)), dma((2 * chunks,)),
                dma((n,)), dma((n,)), dma((kvh,)), dma((kvh,)), dma((kvh,)), dma((kvh,)),
                dma((n,)), dma((n,)), dma((n,)), dma((n,)),
            ],
            compiler_params=pltpu.CompilerParams(
                collective_id=0, has_side_effects=True, vmem_limit_bytes=48 << 20
            ),
        )(
            lengths,
            queries.reshape(steps, kvh, gsize, dim),
            pk.reshape(tokens * kvh, dim),
            pv.reshape(tokens * kvh, dim),
            sk.reshape(suffix * kvh, dim),
            sv.reshape(suffix * kvh, dim),
            nk.reshape(steps, kvh, dim),
            nv.reshape(steps, kvh, dim),
        )
        return out.reshape(1, steps, heads, dim)

    spread = ("group", "sample")
    four = P(spread, None, None, None)
    three = P(spread, None, None)
    return jax.shard_map(
        shards, mesh=mesh,
        in_specs=(four, three, three, four, four, P(spread), four, four),
        out_specs=four, check_vma=False,
    )
```

```python
import functools
import math

import jax
import jax.numpy as jnp
from jax import lax
from jax.experimental import pallas as pl
from jax.experimental.pallas import tpu as pltpu
from jax.sharding import PartitionSpec as P

F32, BF16 = jnp.float32, jnp.bfloat16


def rows_of(tiles):
    wide = tiles.astype(F32)
    return wide.reshape(math.prod(wide.shape[:-1]), wide.shape[-1])


def nt_dot(a, b):
    return lax.dot_general(a, b, (((1,), (1,)), ((), ())), preferred_element_type=F32)


def kernel(
    n, group, chunk,
    len_ref, q_hbm, pk_hbm, pv_hbm, sk_hbm, sv_hbm, nk_hbm, nv_hbm,
    out_ref,
    q_own, pk, pv, wide, k_send, v_send, q_all, k_all, v_all, sk, sv, nk, nv, s_own,
    o_send, l_send, o_all, l_all,
    local_sem, suf_sem, q_ss, q_rs, k_ss, k_rs, v_ss, v_rs, o_ss, o_rs, l_ss, l_rs,
):
    steps, kvh, gsize, dim = q_hbm.shape
    per = steps * gsize
    tokens = pk.shape[0] // kvh
    factor = 1.0 / math.sqrt(dim)
    me = lax.axis_index("sample")
    head = lax.rem(me, kvh)
    base = me - head
    chunks = sk.shape[0] // chunk

    def remote(src, dst, ss, rs, dev):
        return pltpu.make_async_remote_copy(
            src_ref=src, dst_ref=dst, send_sem=ss, recv_sem=rs,
            device_id={"sample": dev}, device_id_type=pl.DeviceIdType.MESH,
        )

    local = [
        pltpu.make_async_copy(a, b, local_sem.at[i])
        for i, (a, b) in enumerate(
            [(pk_hbm, pk), (pv_hbm, pv), (q_hbm, q_own), (nk_hbm, nk), (nv_hbm, nv)]
        )
    ]
    for c in local:
        c.start()
    own_q = pltpu.make_async_copy(q_hbm.at[:, head], q_all.at[me], q_rs.at[me])
    own_q.start()
    halves = []
    for i, (a, b) in enumerate([(sk_hbm, sk), (sv_hbm, sv)]):
        for c in range(chunks):
            part = pl.ds(c * chunk, chunk)
            halves.append(
                pltpu.make_async_copy(a.at[part], b.at[part], suf_sem.at[i * chunks + c])
            )
    for c in halves:
        c.start()

    barrier = pltpu.get_barrier_semaphore()

    def greet(d, _):
        pl.semaphore_signal(
            barrier, inc=1, device_id={"sample": lax.rem(me + d, n)},
            device_id_type=pl.DeviceIdType.MESH,
        )
        return 0

    lax.fori_loop(1, n, greet, 0)

    for src, copy, dst, mine in ((pk, local[0], k_send, k_all), (pv, local[1], v_send, v_all)):
        copy.wait()
        wide[...] = src[...].astype(F32)
        for h in range(kvh):
            dst[h] = wide[pl.ds(h, tokens, stride=kvh), :].astype(BF16)
        mine[head] = wide[pl.ds(head, tokens, stride=kvh), :].astype(BF16)

    pl.semaphore_wait(barrier, n - 1)

    def q_copy(d):
        dev = lax.rem(me + d, n)
        return remote(q_hbm.at[:, lax.rem(dev, kvh)], q_all.at[me], q_ss.at[d], q_rs.at[me], dev)

    def kv_copy(d, src, dst, ss, rs):
        hd = lax.rem(head + d, kvh)
        return remote(src.at[hd], dst.at[head], ss.at[d], rs.at[head], base + hd)

    def start(copy):
        def body(d, _):
            copy(d).start()
            return 0
        return body

    k_copy = lambda d: kv_copy(d, k_send, k_all, k_ss, k_rs)
    v_copy = lambda d: kv_copy(d, v_send, v_all, v_ss, v_rs)
    lax.fori_loop(1, n, start(q_copy), 0)
    lax.fori_loop(1, kvh, start(k_copy), 0)
    lax.fori_loop(1, kvh, start(v_copy), 0)

    for c in local[2:]:
        c.wait()
    rows = kvh * per
    q_rows = jnp.concatenate(
        [q_own[t, h].astype(F32) for h in range(kvh) for t in range(steps)], axis=0
    ).astype(BF16)
    length = len_ref[0]
    row = lax.broadcasted_iota(jnp.int32, (rows, 128), 0)
    lane = lax.broadcasted_iota(jnp.int32, (rows, 128), 1)
    lane_head = lax.rem(lane, kvh)
    match = (row >= lane_head * per) & (row < (lane_head + 1) * per)
    bias = jnp.where(match, 0.0, -jnp.inf).astype(F32)
    bias_wide = jnp.concatenate([bias] * (chunk // 128), axis=1)
    token_of = lax.div(lax.broadcasted_iota(jnp.int32, (8, chunk), 1), kvh)

    top = jnp.full((rows, 1), -jnp.inf, F32)
    for c in range(chunks):
        halves[c].wait()
        s = nt_dot(q_rows, sk[c * chunk:(c + 1) * chunk, :]) * factor
        limit = jnp.where(token_of < length - c * (chunk // kvh), 0.0, -jnp.inf).astype(F32)[:1]
        s = s + bias_wide + limit
        s_own[c] = s
        top = jnp.maximum(top, jnp.max(s, axis=-1, keepdims=True))

    pad = jnp.zeros((128 - steps * kvh, dim), F32)
    new_k = jnp.concatenate([nk[j].astype(F32) for j in range(steps)] + [pad], axis=0).astype(BF16)
    new_v = jnp.concatenate([nv[j].astype(F32) for j in range(steps)] + [pad], axis=0).astype(BF16)
    step_of = lax.div(lax.rem(row, per), gsize)
    s_new = nt_dot(q_rows, new_k) * factor + bias
    s_new = jnp.where(lax.div(lane, kvh) <= step_of, s_new, -jnp.inf)
    own_max = jnp.maximum(top, jnp.max(s_new, axis=-1, keepdims=True))
    w_new = jnp.exp(s_new - own_max)
    own_total = jnp.sum(w_new, axis=-1, keepdims=True)
    own_sum = jnp.dot(w_new.astype(BF16), new_v, preferred_element_type=F32)
    for c in range(chunks):
        halves[chunks + c].wait()
        w = jnp.exp(s_own[c] - own_max)
        own_total = own_total + jnp.sum(w, axis=-1, keepdims=True)
        own_sum = own_sum + jnp.dot(
            w.astype(BF16), sv[c * chunk:(c + 1) * chunk, :], preferred_element_type=F32
        )

    own_q.wait()

    def arrive(make, rs):
        def body(d, _):
            make(d, rs).wait_recv()
            return 0
        return body

    def q_in(d, _):
        src = lax.rem(me + d, n)
        return remote(q_hbm.at[:, head], q_all.at[src], q_ss.at[d], q_rs.at[src], src)

    def kv_in(src, dst, ss, rs):
        def make(d, _):
            hd = lax.rem(head + d, kvh)
            return remote(src.at[hd], dst.at[hd], ss.at[d], rs.at[hd], base + hd)
        return make

    lax.fori_loop(1, n, arrive(q_in, None), 0)
    lax.fori_loop(1, kvh, arrive(kv_in(k_send, k_all, k_ss, k_rs), None), 0)
    lax.fori_loop(1, kvh, arrive(kv_in(v_send, v_all, v_ss, v_rs), None), 0)

    diag_row = lax.broadcasted_iota(jnp.int32, (per, 128), 0)
    diag_lane = lax.broadcasted_iota(jnp.int32, (per, 128), 1)
    diag = diag_row == diag_lane

    def out_copy(dev):
        return remote(o_send.at[dev], o_all.at[me], o_ss.at[dev], o_rs.at[me], dev)

    def log_copy(dev):
        return remote(l_send.at[dev], l_all.at[me], l_ss.at[dev], l_rs.at[me], dev)

    keys = k_all[...].reshape(kvh * tokens, dim)
    values = v_all[...].reshape(kvh * tokens, dim)
    groups = n // group

    def block(i, _):
        first = lax.rem(lax.div(me, group) + 1 + i, groups) * group
        q_block = rows_of(q_all[pl.ds(first, group)]).astype(BF16)
        s = nt_dot(q_block, keys) * factor
        m = jnp.max(s, axis=-1, keepdims=True)
        w = jnp.exp(s - m)
        total = jnp.sum(w, axis=-1, keepdims=True)
        high = w.astype(BF16)
        low = (w - high.astype(F32)).astype(BF16)
        sums = jnp.dot(high, values, preferred_element_type=F32) + jnp.dot(
            low, values, preferred_element_type=F32
        )
        o_send[pl.ds(first, group)] = (sums / total).reshape(group, per, dim)
        logs = jnp.broadcast_to(m + jnp.log(total), (group * per, 128)).reshape(group, per, 128)
        l_send[pl.ds(first, group)] = jnp.sum(
            jnp.where(diag[None], logs, 0.0), axis=1, keepdims=True
        )
        for j in range(group):
            dev = first + j

            @pl.when(dev != me)
            def _():
                out_copy(dev).start()
                log_copy(dev).start()

        return 0

    lax.fori_loop(0, groups, block, 0)
    mine_o = pltpu.make_async_copy(o_send.at[me], o_all.at[me], o_rs.at[me])
    mine_l = pltpu.make_async_copy(l_send.at[me], l_all.at[me], l_rs.at[me])
    mine_o.start()
    mine_l.start()

    def drain(d, _):
        q_copy(d).wait_send()
        return 0

    def drain_kv(d, _):
        k_copy(d).wait_send()
        v_copy(d).wait_send()
        return 0

    lax.fori_loop(1, n, drain, 0)
    lax.fori_loop(1, kvh, drain_kv, 0)
    mine_o.wait()
    mine_l.wait()

    def results_in(d, _):
        src = lax.rem(me + d, n)
        remote(o_send.at[src], o_all.at[src], o_ss.at[src], o_rs.at[src], src).wait_recv()
        remote(l_send.at[src], l_all.at[src], l_ss.at[src], l_rs.at[src], src).wait_recv()
        return 0

    lax.fori_loop(1, n, results_in, 0)

    repeats = n // kvh
    logs = jnp.sum(
        jnp.where(diag[None], jnp.broadcast_to(l_all[...], (n, per, 128)), 0.0),
        axis=-1, keepdims=True,
    ).reshape(repeats, rows, 1)
    largest = jnp.maximum(jnp.max(logs, axis=0), own_max)
    weights = jnp.exp(logs - largest[None])
    share = jnp.exp(own_max - largest)
    upper = share * own_sum
    lower = share * own_total
    for r in range(repeats):
        piece = o_all[r * kvh:(r + 1) * kvh].reshape(rows, dim)
        upper = upper + weights[r] * piece
        lower = lower + weights[r]
    result = upper / lower
    for h in range(kvh):
        for t in range(steps):
            at = h * per + t * gsize
            out_ref[t, h] = result[at:at + gsize]

    def drain_out(d, _):
        dev = lax.rem(me + d, n)
        out_copy(dev).wait_send()
        log_copy(dev).wait_send()
        return 0

    lax.fori_loop(1, n, drain_out, 0)


def solution(mesh):
    n = mesh.shape["sample"]

    def shards(queries, pk, pv, sk, sv, lengths, nk, nv):
        _, steps, heads, dim = queries.shape
        tokens, kvh, _ = pk.shape
        gsize = heads // kvh
        suffix = sk.shape[1]
        per = steps * gsize
        group = math.gcd(n, 4)
        chunk = math.gcd(suffix * kvh, 1024)
        chunks = suffix * kvh // chunk
        any_spec = pl.BlockSpec(memory_space=pl.ANY)
        dma = pltpu.SemaphoreType.DMA
        out = pl.pallas_call(
            functools.partial(kernel, n, group, chunk),
            out_shape=jax.ShapeDtypeStruct((steps, kvh, gsize, dim), F32),
            in_specs=[pl.BlockSpec(memory_space=pltpu.SMEM)] + [any_spec] * 7,
            out_specs=pl.BlockSpec(memory_space=pltpu.VMEM),
            scratch_shapes=[
                pltpu.VMEM((steps, kvh, gsize, dim), BF16),
                pltpu.VMEM((tokens * kvh, dim), BF16),
                pltpu.VMEM((tokens * kvh, dim), BF16),
                pltpu.VMEM((tokens * kvh, dim), F32),
                pltpu.VMEM((kvh, tokens, dim), BF16),
                pltpu.VMEM((kvh, tokens, dim), BF16),
                pltpu.VMEM((n, steps, gsize, dim), BF16),
                pltpu.VMEM((kvh, tokens, dim), BF16),
                pltpu.VMEM((kvh, tokens, dim), BF16),
                pltpu.VMEM((suffix * kvh, dim), BF16),
                pltpu.VMEM((suffix * kvh, dim), BF16),
                pltpu.VMEM((steps, kvh, dim), BF16),
                pltpu.VMEM((steps, kvh, dim), BF16),
                pltpu.VMEM((chunks, kvh * per, chunk), F32),
                pltpu.VMEM((n, per, dim), F32),
                pltpu.VMEM((n, 1, 128), F32),
                pltpu.VMEM((n, per, dim), F32),
                pltpu.VMEM((n, 1, 128), F32),
                dma((5,)), dma((2 * chunks,)),
                dma((n,)), dma((n,)), dma((kvh,)), dma((kvh,)), dma((kvh,)), dma((kvh,)),
                dma((n,)), dma((n,)), dma((n,)), dma((n,)),
            ],
            compiler_params=pltpu.CompilerParams(
                collective_id=0, has_side_effects=True, vmem_limit_bytes=67043328
            ),
        )(
            lengths,
            queries.reshape(steps, kvh, gsize, dim),
            pk.reshape(tokens * kvh, dim),
            pv.reshape(tokens * kvh, dim),
            sk.reshape(suffix * kvh, dim),
            sv.reshape(suffix * kvh, dim),
            nk.reshape(steps, kvh, dim),
            nv.reshape(steps, kvh, dim),
        )
        return out.reshape(1, steps, heads, dim)

    spread = ("group", "sample")
    four = P(spread, None, None, None)
    three = P(spread, None, None)
    return jax.shard_map(
        shards, mesh=mesh,
        in_specs=(four, three, three, four, four, P(spread), four, four),
        out_specs=four, check_vma=False,
    )
```

```python
import functools
import math

import jax
import jax.numpy as jnp
from jax import lax
from jax.experimental import pallas as pl
from jax.experimental.pallas import tpu as pltpu
from jax.sharding import PartitionSpec as P

F32, BF16 = jnp.float32, jnp.bfloat16


def rows_of(tiles):
    wide = tiles.astype(F32)
    return wide.reshape(math.prod(wide.shape[:-1]), wide.shape[-1])


def nt_dot(a, b):
    return lax.dot_general(a, b, (((1,), (1,)), ((), ())), preferred_element_type=F32)


def kernel(
    n, group, chunk,
    len_hbm, q_hbm, pk_hbm, pv_hbm, sk_hbm, sv_hbm, nk_hbm, nv_hbm,
    out_ref,
    q_own, pk, pv, wide, k_send, v_send, q_all, k_all, v_all, sk, sv, nk, nv, s_own,
    o_send, l_send, o_all, l_all, len_own, w_high, w_low, total_all,
    local_sem, suf_sem, q_ss, q_rs, k_ss, k_rs, v_ss, v_rs, o_ss, o_rs, l_ss, l_rs,
):
    steps, kvh, gsize, dim = q_hbm.shape
    per = steps * gsize
    tokens = pk.shape[0] // kvh
    factor = 1.0 / math.sqrt(dim)
    me = lax.axis_index("sample")
    head = lax.rem(me, kvh)
    base = me - head
    chunks = sk.shape[0] // chunk

    def remote(src, dst, ss, rs, dev):
        return pltpu.make_async_remote_copy(
            src_ref=src, dst_ref=dst, send_sem=ss, recv_sem=rs,
            device_id={"sample": dev}, device_id_type=pl.DeviceIdType.MESH,
        )

    local = [
        pltpu.make_async_copy(a, b, local_sem.at[i])
        for i, (a, b) in enumerate(
            [(pk_hbm, pk), (pv_hbm, pv), (q_hbm, q_own), (nk_hbm, nk), (nv_hbm, nv), (len_hbm, len_own)]
        )
    ]
    for c in local:
        c.start()
    own_q = pltpu.make_async_copy(q_hbm.at[:, head], q_all.at[me], q_rs.at[me])
    own_q.start()
    halves = []
    for i, (a, b) in enumerate([(sk_hbm, sk), (sv_hbm, sv)]):
        for c in range(chunks):
            part = pl.ds(c * chunk, chunk)
            halves.append(
                pltpu.make_async_copy(a.at[part], b.at[part], suf_sem.at[i * chunks + c])
            )
    for c in halves:
        c.start()

    barrier = pltpu.get_barrier_semaphore()

    def greet(d, _):
        pl.semaphore_signal(
            barrier, inc=1, device_id={"sample": lax.rem(me + d, n)},
            device_id_type=pl.DeviceIdType.MESH,
        )
        return 0

    lax.fori_loop(1, n, greet, 0)

    for src, copy, dst, mine in ((pk, local[0], k_send, k_all), (pv, local[1], v_send, v_all)):
        copy.wait()
        wide[...] = src[...].astype(F32)
        for h in range(kvh):
            dst[h] = wide[pl.ds(h, tokens, stride=kvh), :].astype(BF16)
        mine[head] = wide[pl.ds(head, tokens, stride=kvh), :].astype(BF16)

    pl.semaphore_wait(barrier, n - 1)

    def q_copy(d):
        dev = lax.rem(me + d, n)
        return remote(q_hbm.at[:, lax.rem(dev, kvh)], q_all.at[me], q_ss.at[d], q_rs.at[me], dev)

    def kv_copy(d, src, dst, ss, rs):
        hd = lax.rem(head + d, kvh)
        return remote(src.at[hd], dst.at[head], ss.at[d], rs.at[head], base + hd)

    def start(copy):
        def body(d, _):
            copy(d).start()
            return 0
        return body

    k_copy = lambda d: kv_copy(d, k_send, k_all, k_ss, k_rs)
    v_copy = lambda d: kv_copy(d, v_send, v_all, v_ss, v_rs)
    lax.fori_loop(1, n, start(q_copy), 0)
    lax.fori_loop(1, kvh, start(k_copy), 0)
    lax.fori_loop(1, kvh, start(v_copy), 0)

    for c in local[2:]:
        c.wait()
    rows = kvh * per
    q_rows = jnp.concatenate(
        [q_own[t, h].astype(F32) for h in range(kvh) for t in range(steps)], axis=0
    ).astype(BF16)
    length = len_own[0]
    row = lax.broadcasted_iota(jnp.int32, (rows, 128), 0)
    lane = lax.broadcasted_iota(jnp.int32, (rows, 128), 1)
    lane_head = lax.rem(lane, kvh)
    match = (row >= lane_head * per) & (row < (lane_head + 1) * per)
    bias = jnp.where(match, 0.0, -jnp.inf).astype(F32)
    bias_wide = jnp.concatenate([bias] * (chunk // 128), axis=1)
    token_of = lax.div(lax.broadcasted_iota(jnp.int32, (8, chunk), 1), kvh)

    top = jnp.full((rows, 1), -jnp.inf, F32)
    for c in range(chunks):
        halves[c].wait()
        s = nt_dot(q_rows, sk[c * chunk:(c + 1) * chunk, :]) * factor
        limit = jnp.where(token_of < length - c * (chunk // kvh), 0.0, -jnp.inf).astype(F32)[:1]
        s = s + bias_wide + limit
        s_own[c] = s
        top = jnp.maximum(top, jnp.max(s, axis=-1, keepdims=True))

    pad = jnp.zeros((128 - steps * kvh, dim), F32)
    new_k = jnp.concatenate([nk[j].astype(F32) for j in range(steps)] + [pad], axis=0).astype(BF16)
    new_v = jnp.concatenate([nv[j].astype(F32) for j in range(steps)] + [pad], axis=0).astype(BF16)
    step_of = lax.div(lax.rem(row, per), gsize)
    s_new = nt_dot(q_rows, new_k) * factor + bias
    s_new = jnp.where(lax.div(lane, kvh) <= step_of, s_new, -jnp.inf)
    own_max = jnp.maximum(top, jnp.max(s_new, axis=-1, keepdims=True))
    w_new = jnp.exp(s_new - own_max)
    own_total = jnp.sum(w_new, axis=-1, keepdims=True)
    own_sum = jnp.dot(w_new.astype(BF16), new_v, preferred_element_type=F32)
    for c in range(chunks):
        halves[chunks + c].wait()
        w = jnp.exp(s_own[c] - own_max)
        own_total = own_total + jnp.sum(w, axis=-1, keepdims=True)
        own_sum = own_sum + jnp.dot(
            w.astype(BF16), sv[c * chunk:(c + 1) * chunk, :], preferred_element_type=F32
        )

    own_q.wait()

    def arrive(make, rs):
        def body(d, _):
            make(d, rs).wait_recv()
            return 0
        return body

    def q_in(d, _):
        src = lax.rem(me + d, n)
        return remote(q_hbm.at[:, head], q_all.at[src], q_ss.at[d], q_rs.at[src], src)

    def kv_in(src, dst, ss, rs):
        def make(d, _):
            hd = lax.rem(head + d, kvh)
            return remote(src.at[hd], dst.at[hd], ss.at[d], rs.at[hd], base + hd)
        return make

    lax.fori_loop(1, n, arrive(q_in, None), 0)
    lax.fori_loop(1, kvh, arrive(kv_in(k_send, k_all, k_ss, k_rs), None), 0)

    diag_row = lax.broadcasted_iota(jnp.int32, (per, 128), 0)
    diag_lane = lax.broadcasted_iota(jnp.int32, (per, 128), 1)
    diag = diag_row == diag_lane

    def out_copy(dev):
        return remote(o_send.at[dev], o_all.at[me], o_ss.at[dev], o_rs.at[me], dev)

    def log_copy(dev):
        return remote(l_send.at[dev], l_all.at[me], l_ss.at[dev], l_rs.at[me], dev)

    keys = k_all[...].reshape(kvh * tokens, dim)
    groups = n // group
    span = group * per

    def first_of(i):
        return lax.rem(lax.div(me, group) + 1 + i, groups) * group

    def weigh(i, _):
        first = first_of(i)
        at = pl.ds(pl.multiple_of(first * per, span), span)
        q_block = rows_of(q_all[pl.ds(first, group)]).astype(BF16)
        s = nt_dot(q_block, keys) * factor
        m = jnp.max(s, axis=-1, keepdims=True)
        w = jnp.exp(s - m)
        total = jnp.sum(w, axis=-1, keepdims=True)
        high = w.astype(BF16)
        w_high[at] = high
        w_low[at] = (w - high.astype(F32)).astype(BF16)
        total_all[at] = total
        logs = jnp.broadcast_to(m + jnp.log(total), (span, 128)).reshape(group, per, 128)
        l_send[pl.ds(first, group)] = jnp.sum(
            jnp.where(diag[None], logs, 0.0), axis=1, keepdims=True
        )
        for j in range(group):
            dev = first + j

            @pl.when(dev != me)
            def _():
                log_copy(dev).start()

        return 0

    lax.fori_loop(0, groups, weigh, 0)
    lax.fori_loop(1, kvh, arrive(kv_in(v_send, v_all, v_ss, v_rs), None), 0)
    values = v_all[...].reshape(kvh * tokens, dim)

    def block(i, _):
        first = first_of(i)
        at = pl.ds(pl.multiple_of(first * per, span), span)
        sums = jnp.dot(w_high[at], values, preferred_element_type=F32) + jnp.dot(
            w_low[at], values, preferred_element_type=F32
        )
        o_send[pl.ds(first, group)] = (sums / total_all[at]).reshape(group, per, dim)
        for j in range(group):
            dev = first + j

            @pl.when(dev != me)
            def _():
                out_copy(dev).start()

        return 0

    lax.fori_loop(0, groups, block, 0)
    mine_o = pltpu.make_async_copy(o_send.at[me], o_all.at[me], o_rs.at[me])
    mine_l = pltpu.make_async_copy(l_send.at[me], l_all.at[me], l_rs.at[me])
    mine_o.start()
    mine_l.start()

    def drain(d, _):
        q_copy(d).wait_send()
        return 0

    def drain_kv(d, _):
        k_copy(d).wait_send()
        v_copy(d).wait_send()
        return 0

    lax.fori_loop(1, n, drain, 0)
    lax.fori_loop(1, kvh, drain_kv, 0)
    mine_o.wait()
    mine_l.wait()

    def results_in(d, _):
        src = lax.rem(me + d, n)
        remote(o_send.at[src], o_all.at[src], o_ss.at[src], o_rs.at[src], src).wait_recv()
        remote(l_send.at[src], l_all.at[src], l_ss.at[src], l_rs.at[src], src).wait_recv()
        return 0

    lax.fori_loop(1, n, results_in, 0)

    repeats = n // kvh
    logs = jnp.sum(
        jnp.where(diag[None], jnp.broadcast_to(l_all[...], (n, per, 128)), 0.0),
        axis=-1, keepdims=True,
    ).reshape(repeats, rows, 1)
    largest = jnp.maximum(jnp.max(logs, axis=0), own_max)
    weights = jnp.exp(logs - largest[None])
    share = jnp.exp(own_max - largest)
    upper = share * own_sum
    lower = share * own_total
    for r in range(repeats):
        piece = o_all[r * kvh:(r + 1) * kvh].reshape(rows, dim)
        upper = upper + weights[r] * piece
        lower = lower + weights[r]
    result = upper / lower
    for h in range(kvh):
        for t in range(steps):
            at = h * per + t * gsize
            out_ref[t, h] = result[at:at + gsize]

    def drain_out(d, _):
        dev = lax.rem(me + d, n)
        out_copy(dev).wait_send()
        log_copy(dev).wait_send()
        return 0

    lax.fori_loop(1, n, drain_out, 0)


def solution(mesh):
    n = mesh.shape["sample"]

    def shards(queries, pk, pv, sk, sv, lengths, nk, nv):
        _, steps, heads, dim = queries.shape
        tokens, kvh, _ = pk.shape
        gsize = heads // kvh
        suffix = sk.shape[1]
        per = steps * gsize
        group = math.gcd(n, 4)
        chunk = math.gcd(suffix * kvh, 1024)
        chunks = suffix * kvh // chunk
        any_spec = pl.BlockSpec(memory_space=pl.ANY)
        dma = pltpu.SemaphoreType.DMA
        out = pl.pallas_call(
            functools.partial(kernel, n, group, chunk),
            out_shape=jax.ShapeDtypeStruct((steps, kvh, gsize, dim), F32),
            in_specs=[any_spec] * 8,
            out_specs=pl.BlockSpec(memory_space=pltpu.VMEM),
            scratch_shapes=[
                pltpu.VMEM((steps, kvh, gsize, dim), BF16),
                pltpu.VMEM((tokens * kvh, dim), BF16),
                pltpu.VMEM((tokens * kvh, dim), BF16),
                pltpu.VMEM((tokens * kvh, dim), F32),
                pltpu.VMEM((kvh, tokens, dim), BF16),
                pltpu.VMEM((kvh, tokens, dim), BF16),
                pltpu.VMEM((n, steps, gsize, dim), BF16),
                pltpu.VMEM((kvh, tokens, dim), BF16),
                pltpu.VMEM((kvh, tokens, dim), BF16),
                pltpu.VMEM((suffix * kvh, dim), BF16),
                pltpu.VMEM((suffix * kvh, dim), BF16),
                pltpu.VMEM((steps, kvh, dim), BF16),
                pltpu.VMEM((steps, kvh, dim), BF16),
                pltpu.VMEM((chunks, kvh * per, chunk), F32),
                pltpu.VMEM((n, per, dim), F32),
                pltpu.VMEM((n, 1, 128), F32),
                pltpu.VMEM((n, per, dim), F32),
                pltpu.VMEM((n, 1, 128), F32),
                pltpu.SMEM((1,), jnp.int32),
                pltpu.VMEM((n * per, kvh * tokens), BF16),
                pltpu.VMEM((n * per, kvh * tokens), BF16),
                pltpu.VMEM((n * per, 1), F32),
                dma((6,)), dma((2 * chunks,)),
                dma((n,)), dma((n,)), dma((kvh,)), dma((kvh,)), dma((kvh,)), dma((kvh,)),
                dma((n,)), dma((n,)), dma((n,)), dma((n,)),
            ],
            compiler_params=pltpu.CompilerParams(
                collective_id=0, has_side_effects=True, vmem_limit_bytes=67043328
            ),
        )(
            lengths,
            queries.reshape(steps, kvh, gsize, dim),
            pk.reshape(tokens * kvh, dim),
            pv.reshape(tokens * kvh, dim),
            sk.reshape(suffix * kvh, dim),
            sv.reshape(suffix * kvh, dim),
            nk.reshape(steps, kvh, dim),
            nv.reshape(steps, kvh, dim),
        )
        return out.reshape(1, steps, heads, dim)

    spread = ("group", "sample")
    four = P(spread, None, None, None)
    three = P(spread, None, None)
    return jax.shard_map(
        shards, mesh=mesh,
        in_specs=(four, three, three, four, four, P(spread), four, four),
        out_specs=four, check_vma=False,
    )
```

```python
import functools
import math

import jax
import jax.numpy as jnp
from jax import lax
from jax.experimental import pallas as pl
from jax.experimental.pallas import tpu as pltpu
from jax.sharding import PartitionSpec as P

F32, BF16 = jnp.float32, jnp.bfloat16


def rows_of(tiles):
    wide = tiles.astype(F32)
    return wide.reshape(math.prod(wide.shape[:-1]), wide.shape[-1])


def nt_dot(a, b):
    return lax.dot_general(a, b, (((1,), (1,)), ((), ())), preferred_element_type=F32)


def kernel(
    n, group, chunk,
    len_hbm, q_hbm, pk_hbm, pv_hbm, sk_hbm, sv_hbm, nk_hbm, nv_hbm,
    out_ref,
    q_own, pk, pv, wide, k_send, v_send, q_all, k_all, v_all, sk, sv, nk, nv, s_own,
    o_send, l_send, o_all, l_all, len_own, w_high, w_low, total_all, q_far,
    local_sem, suf_sem, q_ss, q_rs, f_ss, f_rs, k_ss, k_rs, v_ss, v_rs, o_ss, o_rs, l_ss, l_rs,
):
    steps, kvh, gsize, dim = q_hbm.shape
    per = steps * gsize
    tokens = pk.shape[0] // kvh
    factor = 1.0 / math.sqrt(dim)
    me = lax.axis_index("sample")
    head = lax.rem(me, kvh)
    base = me - head
    blk = lax.div(me, kvh)
    blocks = n // kvh
    chunks = sk.shape[0] // chunk

    def remote(src, dst, ss, rs, dev):
        return pltpu.make_async_remote_copy(
            src_ref=src, dst_ref=dst, send_sem=ss, recv_sem=rs,
            device_id={"sample": dev}, device_id_type=pl.DeviceIdType.MESH,
        )

    local = [
        pltpu.make_async_copy(a, b, local_sem.at[i])
        for i, (a, b) in enumerate(
            [(pk_hbm, pk), (pv_hbm, pv), (q_hbm, q_own), (nk_hbm, nk), (nv_hbm, nv), (len_hbm, len_own)]
        )
    ]
    for c in local:
        c.start()
    own_q = pltpu.make_async_copy(q_hbm.at[:, head], q_all.at[me], q_rs.at[me])
    own_q.start()
    halves = []
    for i, (a, b) in enumerate([(sk_hbm, sk), (sv_hbm, sv)]):
        for c in range(chunks):
            part = pl.ds(c * chunk, chunk)
            halves.append(
                pltpu.make_async_copy(a.at[part], b.at[part], suf_sem.at[i * chunks + c])
            )
    for c in halves:
        c.start()

    barrier = pltpu.get_barrier_semaphore()

    def greet(dev):
        pl.semaphore_signal(
            barrier, inc=1, device_id={"sample": dev}, device_id_type=pl.DeviceIdType.MESH
        )

    for d in range(1, kvh):
        greet(base + lax.rem(head + d, kvh))

    def greet_far(e, _):
        greet(lax.rem(blk + e, blocks) * kvh + head)
        return 0

    lax.fori_loop(1, blocks, greet_far, 0)

    for src, copy, dst, mine in ((pk, local[0], k_send, k_all), (pv, local[1], v_send, v_all)):
        copy.wait()
        wide[...] = src[...].astype(F32)
        for h in range(kvh):
            dst[h] = wide[pl.ds(h, tokens, stride=kvh), :].astype(BF16)
        mine[head] = wide[pl.ds(head, tokens, stride=kvh), :].astype(BF16)

    pl.semaphore_wait(barrier, kvh + blocks - 2)

    def far_copy(e):
        dev = lax.rem(blk + e, blocks) * kvh + head
        return remote(q_hbm, q_far.at[blk], f_ss.at[e], f_rs.at[blk], dev)

    def far_in(e):
        r = lax.rem(blk + e, blocks)
        return remote(q_hbm, q_far.at[r], f_ss.at[e], f_rs.at[r], r * kvh + head)

    def q_copy(e, d):
        hd = lax.rem(head + d, kvh)
        r = lax.rem(blk + e, blocks)
        at = r * kvh + head
        src = q_hbm if isinstance(e, int) else q_far.at[r]
        return remote(src.at[:, hd], q_all.at[at], q_ss.at[e * kvh + d], q_rs.at[at], base + hd)

    def q_keep(e):
        r = lax.rem(blk + e, blocks)
        at = r * kvh + head
        return pltpu.make_async_copy(q_far.at[r, :, head], q_all.at[at], q_rs.at[at])

    def q_in(e, d):
        hd = lax.rem(head + d, kvh)
        at = lax.rem(blk + e, blocks) * kvh + hd
        return remote(
            q_hbm.at[:, head], q_all.at[at], q_ss.at[e * kvh + d], q_rs.at[at], base + hd
        )

    def kv_copy(d, src, dst, ss, rs):
        hd = lax.rem(head + d, kvh)
        return remote(src.at[hd], dst.at[head], ss.at[d], rs.at[head], base + hd)

    def start(copy):
        def body(d, _):
            copy(d).start()
            return 0
        return body

    k_copy = lambda d: kv_copy(d, k_send, k_all, k_ss, k_rs)
    v_copy = lambda d: kv_copy(d, v_send, v_all, v_ss, v_rs)
    lax.fori_loop(1, blocks, start(far_copy), 0)
    for d in range(1, kvh):
        q_copy(0, d).start()
    lax.fori_loop(1, kvh, start(k_copy), 0)

    for c in local[2:]:
        c.wait()
    rows = kvh * per
    q_rows = jnp.concatenate(
        [q_own[t, h].astype(F32) for h in range(kvh) for t in range(steps)], axis=0
    ).astype(BF16)
    length = len_own[0]
    row = lax.broadcasted_iota(jnp.int32, (rows, 128), 0)
    lane = lax.broadcasted_iota(jnp.int32, (rows, 128), 1)
    lane_head = lax.rem(lane, kvh)
    match = (row >= lane_head * per) & (row < (lane_head + 1) * per)
    bias = jnp.where(match, 0.0, -jnp.inf).astype(F32)
    bias_wide = jnp.concatenate([bias] * (chunk // 128), axis=1)
    token_of = lax.div(lax.broadcasted_iota(jnp.int32, (8, chunk), 1), kvh)

    top = jnp.full((rows, 1), -jnp.inf, F32)
    for c in range(chunks):
        halves[c].wait()
        s = nt_dot(q_rows, sk[c * chunk:(c + 1) * chunk, :]) * factor
        limit = jnp.where(token_of < length - c * (chunk // kvh), 0.0, -jnp.inf).astype(F32)[:1]
        s = s + bias_wide + limit
        s_own[c] = s
        top = jnp.maximum(top, jnp.max(s, axis=-1, keepdims=True))

    def hand_on(e, _):
        far_in(e).wait_recv()
        for d in range(1, kvh):
            q_copy(e, d).start()
        q_keep(e).start()
        return 0

    lax.fori_loop(1, blocks, hand_on, 0)
    lax.fori_loop(1, kvh, start(v_copy), 0)

    pad = jnp.zeros((128 - steps * kvh, dim), F32)
    new_k = jnp.concatenate([nk[j].astype(F32) for j in range(steps)] + [pad], axis=0).astype(BF16)
    new_v = jnp.concatenate([nv[j].astype(F32) for j in range(steps)] + [pad], axis=0).astype(BF16)
    step_of = lax.div(lax.rem(row, per), gsize)
    s_new = nt_dot(q_rows, new_k) * factor + bias
    s_new = jnp.where(lax.div(lane, kvh) <= step_of, s_new, -jnp.inf)
    own_max = jnp.maximum(top, jnp.max(s_new, axis=-1, keepdims=True))
    w_new = jnp.exp(s_new - own_max)
    own_total = jnp.sum(w_new, axis=-1, keepdims=True)
    own_sum = jnp.dot(w_new.astype(BF16), new_v, preferred_element_type=F32)
    for c in range(chunks):
        halves[chunks + c].wait()
        w = jnp.exp(s_own[c] - own_max)
        own_total = own_total + jnp.sum(w, axis=-1, keepdims=True)
        own_sum = own_sum + jnp.dot(
            w.astype(BF16), sv[c * chunk:(c + 1) * chunk, :], preferred_element_type=F32
        )

    own_q.wait()

    def arrive(make, rs):
        def body(d, _):
            make(d, rs).wait_recv()
            return 0
        return body

    def kv_in(src, dst, ss, rs):
        def make(d, _):
            hd = lax.rem(head + d, kvh)
            return remote(src.at[hd], dst.at[hd], ss.at[d], rs.at[hd], base + hd)
        return make

    for d in range(1, kvh):
        q_in(0, d).wait_recv()

    def far_q_in(e, _):
        for d in range(1, kvh):
            q_in(e, d).wait_recv()
        q_keep(e).wait()
        return 0

    lax.fori_loop(1, blocks, far_q_in, 0)
    lax.fori_loop(1, kvh, arrive(kv_in(k_send, k_all, k_ss, k_rs), None), 0)

    diag_row = lax.broadcasted_iota(jnp.int32, (per, 128), 0)
    diag_lane = lax.broadcasted_iota(jnp.int32, (per, 128), 1)
    diag = diag_row == diag_lane

    def out_copy(dev):
        return remote(o_send.at[dev], o_all.at[me], o_ss.at[dev], o_rs.at[me], dev)

    def log_copy(dev):
        return remote(l_send.at[dev], l_all.at[me], l_ss.at[dev], l_rs.at[me], dev)

    keys = k_all[...].reshape(kvh * tokens, dim)
    groups = n // group
    span = group * per

    def first_of(i):
        return lax.rem(base + kvh + i * group, n)

    def weigh(i, _):
        first = first_of(i)
        at = pl.ds(pl.multiple_of(first * per, span), span)
        q_block = rows_of(q_all[pl.ds(first, group)]).astype(BF16)
        s = nt_dot(q_block, keys) * factor
        m = jnp.max(s, axis=-1, keepdims=True)
        w = jnp.exp(s - m)
        total = jnp.sum(w, axis=-1, keepdims=True)
        high = w.astype(BF16)
        w_high[at] = high
        w_low[at] = (w - high.astype(F32)).astype(BF16)
        total_all[at] = total
        logs = jnp.broadcast_to(m + jnp.log(total), (span, 128)).reshape(group, per, 128)
        l_send[pl.ds(first, group)] = jnp.sum(
            jnp.where(diag[None], logs, 0.0), axis=1, keepdims=True
        )
        for j in range(group):
            dev = first + j

            @pl.when(dev != me)
            def _():
                log_copy(dev).start()

        return 0

    lax.fori_loop(0, groups, weigh, 0)
    lax.fori_loop(1, kvh, arrive(kv_in(v_send, v_all, v_ss, v_rs), None), 0)
    values = v_all[...].reshape(kvh * tokens, dim)

    def block(i, _):
        first = first_of(i)
        at = pl.ds(pl.multiple_of(first * per, span), span)
        sums = jnp.dot(w_high[at], values, preferred_element_type=F32) + jnp.dot(
            w_low[at], values, preferred_element_type=F32
        )
        o_send[pl.ds(first, group)] = (sums / total_all[at]).reshape(group, per, dim)
        for j in range(group):
            dev = first + j

            @pl.when(dev != me)
            def _():
                out_copy(dev).start()

        return 0

    lax.fori_loop(0, groups, block, 0)
    mine_o = pltpu.make_async_copy(o_send.at[me], o_all.at[me], o_rs.at[me])
    mine_l = pltpu.make_async_copy(l_send.at[me], l_all.at[me], l_rs.at[me])
    mine_o.start()
    mine_l.start()

    for d in range(1, kvh):
        q_copy(0, d).wait_send()

    def drain(e, _):
        far_copy(e).wait_send()
        for d in range(1, kvh):
            q_copy(e, d).wait_send()
        return 0

    def drain_kv(d, _):
        k_copy(d).wait_send()
        v_copy(d).wait_send()
        return 0

    lax.fori_loop(1, blocks, drain, 0)
    lax.fori_loop(1, kvh, drain_kv, 0)
    mine_o.wait()
    mine_l.wait()

    def results_in(d, _):
        src = lax.rem(me + d, n)
        remote(o_send.at[src], o_all.at[src], o_ss.at[src], o_rs.at[src], src).wait_recv()
        remote(l_send.at[src], l_all.at[src], l_ss.at[src], l_rs.at[src], src).wait_recv()
        return 0

    lax.fori_loop(1, n, results_in, 0)

    repeats = n // kvh
    logs = jnp.sum(
        jnp.where(diag[None], jnp.broadcast_to(l_all[...], (n, per, 128)), 0.0),
        axis=-1, keepdims=True,
    ).reshape(repeats, rows, 1)
    largest = jnp.maximum(jnp.max(logs, axis=0), own_max)
    weights = jnp.exp(logs - largest[None])
    share = jnp.exp(own_max - largest)
    upper = share * own_sum
    lower = share * own_total
    for r in range(repeats):
        piece = o_all[r * kvh:(r + 1) * kvh].reshape(rows, dim)
        upper = upper + weights[r] * piece
        lower = lower + weights[r]
    result = upper / lower
    for h in range(kvh):
        for t in range(steps):
            at = h * per + t * gsize
            out_ref[t, h] = result[at:at + gsize]

    def drain_out(d, _):
        dev = lax.rem(me + d, n)
        out_copy(dev).wait_send()
        log_copy(dev).wait_send()
        return 0

    lax.fori_loop(1, n, drain_out, 0)


def solution(mesh):
    n = mesh.shape["sample"]

    def shards(queries, pk, pv, sk, sv, lengths, nk, nv):
        _, steps, heads, dim = queries.shape
        tokens, kvh, _ = pk.shape
        gsize = heads // kvh
        suffix = sk.shape[1]
        per = steps * gsize
        group = math.gcd(kvh, 4)
        blocks = n // kvh
        chunk = math.gcd(suffix * kvh, 1024)
        chunks = suffix * kvh // chunk
        any_spec = pl.BlockSpec(memory_space=pl.ANY)
        dma = pltpu.SemaphoreType.DMA
        out = pl.pallas_call(
            functools.partial(kernel, n, group, chunk),
            out_shape=jax.ShapeDtypeStruct((steps, kvh, gsize, dim), F32),
            in_specs=[any_spec] * 8,
            out_specs=pl.BlockSpec(memory_space=pltpu.VMEM),
            scratch_shapes=[
                pltpu.VMEM((steps, kvh, gsize, dim), BF16),
                pltpu.VMEM((tokens * kvh, dim), BF16),
                pltpu.VMEM((tokens * kvh, dim), BF16),
                pltpu.VMEM((tokens * kvh, dim), F32),
                pltpu.VMEM((kvh, tokens, dim), BF16),
                pltpu.VMEM((kvh, tokens, dim), BF16),
                pltpu.VMEM((n, steps, gsize, dim), BF16),
                pltpu.VMEM((kvh, tokens, dim), BF16),
                pltpu.VMEM((kvh, tokens, dim), BF16),
                pltpu.VMEM((suffix * kvh, dim), BF16),
                pltpu.VMEM((suffix * kvh, dim), BF16),
                pltpu.VMEM((steps, kvh, dim), BF16),
                pltpu.VMEM((steps, kvh, dim), BF16),
                pltpu.VMEM((chunks, kvh * per, chunk), F32),
                pltpu.VMEM((n, per, dim), F32),
                pltpu.VMEM((n, 1, 128), F32),
                pltpu.VMEM((n, per, dim), F32),
                pltpu.VMEM((n, 1, 128), F32),
                pltpu.SMEM((1,), jnp.int32),
                pltpu.VMEM((n * per, kvh * tokens), BF16),
                pltpu.VMEM((n * per, kvh * tokens), BF16),
                pltpu.VMEM((n * per, 1), F32),
                pltpu.VMEM((blocks, steps, kvh, gsize, dim), BF16),
                dma((6,)), dma((2 * chunks,)),
                dma((n,)), dma((n,)), dma((blocks,)), dma((blocks,)), dma((kvh,)), dma((kvh,)), dma((kvh,)), dma((kvh,)),
                dma((n,)), dma((n,)), dma((n,)), dma((n,)),
            ],
            compiler_params=pltpu.CompilerParams(
                collective_id=0, has_side_effects=True, vmem_limit_bytes=67043328
            ),
        )(
            lengths,
            queries.reshape(steps, kvh, gsize, dim),
            pk.reshape(tokens * kvh, dim),
            pv.reshape(tokens * kvh, dim),
            sk.reshape(suffix * kvh, dim),
            sv.reshape(suffix * kvh, dim),
            nk.reshape(steps, kvh, dim),
            nv.reshape(steps, kvh, dim),
        )
        return out.reshape(1, steps, heads, dim)

    spread = ("group", "sample")
    four = P(spread, None, None, None)
    three = P(spread, None, None)
    return jax.shard_map(
        shards, mesh=mesh,
        in_specs=(four, three, three, four, four, P(spread), four, four),
        out_specs=four, check_vma=False,
    )
```

```python
import functools
import math

import jax
import jax.numpy as jnp
from jax import lax
from jax.experimental import pallas as pl
from jax.experimental.pallas import tpu as pltpu
from jax.sharding import PartitionSpec as P

F32, BF16 = jnp.float32, jnp.bfloat16


def rows_of(tiles):
    wide = tiles.astype(F32)
    return wide.reshape(math.prod(wide.shape[:-1]), wide.shape[-1])


def nt_dot(a, b):
    return lax.dot_general(a, b, (((1,), (1,)), ((), ())), preferred_element_type=F32)


def kernel(
    n, group, chunk,
    len_hbm, q_hbm, pk_hbm, pv_hbm, sk_hbm, sv_hbm, nk_hbm, nv_hbm,
    out_ref,
    q_own, pk, pv, wide, k_send, v_send, q_all, k_all, v_all, sk, sv, nk, nv, s_own,
    o_send, l_send, o_all, l_all, len_own, w_high, w_low, total_all,
    local_sem, suf_sem, q_ss, q_rs, k_ss, k_rs, v_ss, v_rs, o_ss, o_rs, l_ss, l_rs,
):
    steps, kvh, gsize, dim = q_hbm.shape
    per = steps * gsize
    tokens = pk.shape[0] // kvh
    factor = 1.0 / math.sqrt(dim)
    me = lax.axis_index("sample")
    head = lax.rem(me, kvh)
    base = me - head
    chunks = sk.shape[0] // chunk

    def remote(src, dst, ss, rs, dev):
        return pltpu.make_async_remote_copy(
            src_ref=src, dst_ref=dst, send_sem=ss, recv_sem=rs,
            device_id={"sample": dev}, device_id_type=pl.DeviceIdType.MESH,
        )

    local = [
        pltpu.make_async_copy(a, b, local_sem.at[i])
        for i, (a, b) in enumerate(
            [(pk_hbm, pk), (pv_hbm, pv), (q_hbm, q_own), (nk_hbm, nk), (nv_hbm, nv), (len_hbm, len_own)]
        )
    ]
    for c in local:
        c.start()
    own_q = pltpu.make_async_copy(q_hbm.at[:, head], q_all.at[me], q_rs.at[me])
    own_q.start()
    halves = []
    for i, (a, b) in enumerate([(sk_hbm, sk), (sv_hbm, sv)]):
        for c in range(chunks):
            part = pl.ds(c * chunk, chunk)
            halves.append(
                pltpu.make_async_copy(a.at[part], b.at[part], suf_sem.at[i * chunks + c])
            )
    for c in halves:
        c.start()

    barrier = pltpu.get_barrier_semaphore()

    def greet(d, _):
        pl.semaphore_signal(
            barrier, inc=1, device_id={"sample": lax.rem(me + d, n)},
            device_id_type=pl.DeviceIdType.MESH,
        )
        return 0

    lax.fori_loop(1, n, greet, 0)

    for src, copy, dst, mine in ((pk, local[0], k_send, k_all), (pv, local[1], v_send, v_all)):
        copy.wait()
        wide[...] = src[...].astype(F32)
        for h in range(kvh):
            dst[h] = wide[pl.ds(h, tokens, stride=kvh), :].astype(BF16)
        mine[head] = wide[pl.ds(head, tokens, stride=kvh), :].astype(BF16)

    pl.semaphore_wait(barrier, n - 1)

    def q_copy(d):
        dev = lax.rem(me + d, n)
        return remote(q_hbm.at[:, lax.rem(dev, kvh)], q_all.at[me], q_ss.at[d], q_rs.at[me], dev)

    def kv_copy(d, src, dst, ss, rs):
        hd = lax.rem(head + d, kvh)
        return remote(src.at[hd], dst.at[head], ss.at[d], rs.at[head], base + hd)

    def start(copy):
        def body(d, _):
            copy(d).start()
            return 0
        return body

    k_copy = lambda d: kv_copy(d, k_send, k_all, k_ss, k_rs)
    v_copy = lambda d: kv_copy(d, v_send, v_all, v_ss, v_rs)
    lax.fori_loop(1, n, start(q_copy), 0)
    lax.fori_loop(1, kvh, start(k_copy), 0)
    lax.fori_loop(1, kvh, start(v_copy), 0)

    for c in local[2:]:
        c.wait()
    rows = kvh * per
    q_rows = jnp.concatenate(
        [q_own[t, h].astype(F32) for h in range(kvh) for t in range(steps)], axis=0
    ).astype(BF16)
    length = len_own[0]
    row = lax.broadcasted_iota(jnp.int32, (rows, 128), 0)
    lane = lax.broadcasted_iota(jnp.int32, (rows, 128), 1)
    lane_head = lax.rem(lane, kvh)
    match = (row >= lane_head * per) & (row < (lane_head + 1) * per)
    bias = jnp.where(match, 0.0, -jnp.inf).astype(F32)
    bias_wide = jnp.concatenate([bias] * (chunk // 128), axis=1)
    token_of = lax.div(lax.broadcasted_iota(jnp.int32, (8, chunk), 1), kvh)

    top = jnp.full((rows, 1), -jnp.inf, F32)
    for c in range(chunks):
        halves[c].wait()
        s = nt_dot(q_rows, sk[c * chunk:(c + 1) * chunk, :]) * factor
        limit = jnp.where(token_of < length - c * (chunk // kvh), 0.0, -jnp.inf).astype(F32)[:1]
        s = s + bias_wide + limit
        s_own[c] = s
        top = jnp.maximum(top, jnp.max(s, axis=-1, keepdims=True))

    pad = jnp.zeros((128 - steps * kvh, dim), F32)
    new_k = jnp.concatenate([nk[j].astype(F32) for j in range(steps)] + [pad], axis=0).astype(BF16)
    new_v = jnp.concatenate([nv[j].astype(F32) for j in range(steps)] + [pad], axis=0).astype(BF16)
    step_of = lax.div(lax.rem(row, per), gsize)
    s_new = nt_dot(q_rows, new_k) * factor + bias
    s_new = jnp.where(lax.div(lane, kvh) <= step_of, s_new, -jnp.inf)
    own_max = jnp.maximum(top, jnp.max(s_new, axis=-1, keepdims=True))
    w_new = jnp.exp(s_new - own_max)
    own_total = jnp.sum(w_new, axis=-1, keepdims=True)
    own_sum = jnp.dot(w_new.astype(BF16), new_v, preferred_element_type=F32)
    for c in range(chunks):
        halves[chunks + c].wait()
        w = jnp.exp(s_own[c] - own_max)
        own_total = own_total + jnp.sum(w, axis=-1, keepdims=True)
        own_sum = own_sum + jnp.dot(
            w.astype(BF16), sv[c * chunk:(c + 1) * chunk, :], preferred_element_type=F32
        )

    own_q.wait()

    def arrive(make, rs):
        def body(d, _):
            make(d, rs).wait_recv()
            return 0
        return body

    def q_in(d, _):
        src = lax.rem(me + d, n)
        return remote(q_hbm.at[:, head], q_all.at[src], q_ss.at[d], q_rs.at[src], src)

    def kv_in(src, dst, ss, rs):
        def make(d, _):
            hd = lax.rem(head + d, kvh)
            return remote(src.at[hd], dst.at[hd], ss.at[d], rs.at[hd], base + hd)
        return make

    lax.fori_loop(1, n, arrive(q_in, None), 0)
    lax.fori_loop(1, kvh, arrive(kv_in(k_send, k_all, k_ss, k_rs), None), 0)

    diag_row = lax.broadcasted_iota(jnp.int32, (per, 128), 0)
    diag_lane = lax.broadcasted_iota(jnp.int32, (per, 128), 1)
    diag = diag_row == diag_lane

    def out_copy(dev):
        return remote(o_send.at[dev], o_all.at[me], o_ss.at[dev], o_rs.at[me], dev)

    def log_copy(dev):
        return remote(l_send.at[dev], l_all.at[me], l_ss.at[dev], l_rs.at[me], dev)

    keys = k_all[...].reshape(kvh * tokens, dim)
    groups = n // group
    span = group * per

    def first_of(i):
        return lax.rem(lax.div(me, group) + 1 + i, groups) * group

    def weigh(i, _):
        first = first_of(i)
        at = pl.ds(pl.multiple_of(first * per, span), span)
        q_block = rows_of(q_all[pl.ds(first, group)]).astype(BF16)
        s = nt_dot(q_block, keys) * factor
        m = jnp.max(s, axis=-1, keepdims=True)
        w = jnp.exp(s - m)
        total = jnp.sum(w, axis=-1, keepdims=True)
        high = w.astype(BF16)
        w_high[at] = high
        w_low[at] = (w - high.astype(F32)).astype(BF16)
        total_all[at] = total
        logs = jnp.broadcast_to(m + jnp.log(total), (span, 128)).reshape(group, per, 128)
        l_send[pl.ds(first, group)] = jnp.sum(
            jnp.where(diag[None], logs, 0.0), axis=1, keepdims=True
        )
        for j in range(group):
            dev = first + j

            @pl.when(dev != me)
            def _():
                log_copy(dev).start()

        return 0

    lax.fori_loop(0, groups, weigh, 0)
    lax.fori_loop(1, kvh, arrive(kv_in(v_send, v_all, v_ss, v_rs), None), 0)
    values = v_all[...].reshape(kvh * tokens, dim)

    def block(i, _):
        first = first_of(i)
        at = pl.ds(pl.multiple_of(first * per, span), span)
        sums = jnp.dot(w_high[at], values, preferred_element_type=F32) + jnp.dot(
            w_low[at], values, preferred_element_type=F32
        )
        o_send[pl.ds(first, group)] = (sums / total_all[at]).reshape(group, per, dim)
        for j in range(group):
            dev = first + j

            @pl.when(dev != me)
            def _():
                out_copy(dev).start()

        return 0

    lax.fori_loop(0, groups, block, 0)
    mine_o = pltpu.make_async_copy(o_send.at[me], o_all.at[me], o_rs.at[me])
    mine_l = pltpu.make_async_copy(l_send.at[me], l_all.at[me], l_rs.at[me])
    mine_o.start()
    mine_l.start()

    def drain(d, _):
        q_copy(d).wait_send()
        return 0

    def drain_kv(d, _):
        k_copy(d).wait_send()
        v_copy(d).wait_send()
        return 0

    lax.fori_loop(1, n, drain, 0)
    lax.fori_loop(1, kvh, drain_kv, 0)
    mine_o.wait()
    mine_l.wait()

    def results_in(d, _):
        src = lax.rem(me + d, n)
        remote(o_send.at[src], o_all.at[src], o_ss.at[src], o_rs.at[src], src).wait_recv()
        remote(l_send.at[src], l_all.at[src], l_ss.at[src], l_rs.at[src], src).wait_recv()
        return 0

    lax.fori_loop(1, n, results_in, 0)

    repeats = n // kvh
    logs = jnp.sum(
        jnp.where(diag[None], jnp.broadcast_to(l_all[...], (n, per, 128)), 0.0),
        axis=-1, keepdims=True,
    ).reshape(repeats, rows, 1)
    largest = jnp.maximum(jnp.max(logs, axis=0), own_max)
    weights = jnp.exp(logs - largest[None])
    share = jnp.exp(own_max - largest)
    upper = share * own_sum
    lower = share * own_total
    for r in range(repeats):
        piece = o_all[r * kvh:(r + 1) * kvh].reshape(rows, dim)
        upper = upper + weights[r] * piece
        lower = lower + weights[r]
    result = upper / lower
    for h in range(kvh):
        for t in range(steps):
            at = h * per + t * gsize
            out_ref[t, h] = result[at:at + gsize]

    def drain_out(d, _):
        dev = lax.rem(me + d, n)
        out_copy(dev).wait_send()
        log_copy(dev).wait_send()
        return 0

    lax.fori_loop(1, n, drain_out, 0)


def solution(mesh):
    n = mesh.shape["sample"]

    def shards(queries, pk, pv, sk, sv, lengths, nk, nv):
        _, steps, heads, dim = queries.shape
        tokens, kvh, _ = pk.shape
        gsize = heads // kvh
        suffix = sk.shape[1]
        per = steps * gsize
        group = math.gcd(n, 4)
        chunk = math.gcd(suffix * kvh, 1024)
        chunks = suffix * kvh // chunk
        any_spec = pl.BlockSpec(memory_space=pl.ANY)
        dma = pltpu.SemaphoreType.DMA
        out = pl.pallas_call(
            functools.partial(kernel, n, group, chunk),
            out_shape=jax.ShapeDtypeStruct((steps, kvh, gsize, dim), F32),
            in_specs=[any_spec] + [pl.BlockSpec(memory_space=pltpu.HBM)] * 7,
            out_specs=pl.BlockSpec(memory_space=pltpu.VMEM),
            scratch_shapes=[
                pltpu.VMEM((steps, kvh, gsize, dim), BF16),
                pltpu.VMEM((tokens * kvh, dim), BF16),
                pltpu.VMEM((tokens * kvh, dim), BF16),
                pltpu.VMEM((tokens * kvh, dim), F32),
                pltpu.VMEM((kvh, tokens, dim), BF16),
                pltpu.VMEM((kvh, tokens, dim), BF16),
                pltpu.VMEM((n, steps, gsize, dim), BF16),
                pltpu.VMEM((kvh, tokens, dim), BF16),
                pltpu.VMEM((kvh, tokens, dim), BF16),
                pltpu.VMEM((suffix * kvh, dim), BF16),
                pltpu.VMEM((suffix * kvh, dim), BF16),
                pltpu.VMEM((steps, kvh, dim), BF16),
                pltpu.VMEM((steps, kvh, dim), BF16),
                pltpu.VMEM((chunks, kvh * per, chunk), F32),
                pltpu.VMEM((n, per, dim), F32),
                pltpu.VMEM((n, 1, 128), F32),
                pltpu.VMEM((n, per, dim), F32),
                pltpu.VMEM((n, 1, 128), F32),
                pltpu.SMEM((1,), jnp.int32),
                pltpu.VMEM((n * per, kvh * tokens), BF16),
                pltpu.VMEM((n * per, kvh * tokens), BF16),
                pltpu.VMEM((n * per, 1), F32),
                dma((6,)), dma((2 * chunks,)),
                dma((n,)), dma((n,)), dma((kvh,)), dma((kvh,)), dma((kvh,)), dma((kvh,)),
                dma((n,)), dma((n,)), dma((n,)), dma((n,)),
            ],
            compiler_params=pltpu.CompilerParams(
                collective_id=0, has_side_effects=True, vmem_limit_bytes=48 << 20
            ),
        )(lengths, *[pltpu.with_memory_space_constraint(x, pltpu.HBM) for x in (
            queries.reshape(steps, kvh, gsize, dim),
            pk.reshape(tokens * kvh, dim),
            pv.reshape(tokens * kvh, dim),
            sk.reshape(suffix * kvh, dim),
            sv.reshape(suffix * kvh, dim),
            nk.reshape(steps, kvh, dim),
            nv.reshape(steps, kvh, dim),
        )])
        return out.reshape(1, steps, heads, dim)

    spread = ("group", "sample")
    four = P(spread, None, None, None)
    three = P(spread, None, None)
    return jax.shard_map(
        shards, mesh=mesh,
        in_specs=(four, three, three, four, four, P(spread), four, four),
        out_specs=four, check_vma=False,
    )
```

```python
import functools
import math

import jax
import jax.numpy as jnp
from jax import lax
from jax.experimental import pallas as pl
from jax.experimental.pallas import tpu as pltpu
from jax.sharding import PartitionSpec as P

F32, BF16 = jnp.float32, jnp.bfloat16


def rows_of(tiles):
    wide = tiles.astype(F32)
    return wide.reshape(math.prod(wide.shape[:-1]), wide.shape[-1])


def nt_dot(a, b):
    return lax.dot_general(a, b, (((1,), (1,)), ((), ())), preferred_element_type=F32)


def kernel(
    n, group, chunk,
    len_hbm, q_hbm, pk_hbm, pv_hbm, sk_hbm, sv_hbm, nk_hbm, nv_hbm,
    out_ref,
    q_own, pk, pv, wide, k_send, v_send, q_all, k_all, v_all, sk, sv, nk, nv, s_own,
    o_send, l_send, o_all, l_all, len_own, w_high, w_low, total_all,
    local_sem, suf_sem, q_ss, q_rs, k_ss, k_rs, v_ss, v_rs, o_ss, o_rs, l_ss, l_rs,
):
    steps, kvh, gsize, dim = q_hbm.shape
    per = steps * gsize
    tokens = pk.shape[0] // kvh
    factor = 1.0 / math.sqrt(dim)
    me = lax.axis_index("sample")
    head = lax.rem(me, kvh)
    base = me - head
    chunks = sk.shape[0] // chunk

    def remote(src, dst, ss, rs, dev):
        return pltpu.make_async_remote_copy(
            src_ref=src, dst_ref=dst, send_sem=ss, recv_sem=rs,
            device_id={"sample": dev}, device_id_type=pl.DeviceIdType.MESH,
        )

    local = [
        pltpu.make_async_copy(a, b, local_sem.at[i])
        for i, (a, b) in enumerate(
            [(pk_hbm, pk), (pv_hbm, pv), (q_hbm, q_own), (nk_hbm, nk), (nv_hbm, nv), (len_hbm, len_own)]
        )
    ]
    for c in local:
        c.start()
    own_q = pltpu.make_async_copy(q_hbm.at[:, head], q_all.at[me], q_rs.at[me])
    own_q.start()
    halves = []
    for i, (a, b) in enumerate([(sk_hbm, sk), (sv_hbm, sv)]):
        for c in range(chunks):
            part = pl.ds(c * chunk, chunk)
            halves.append(
                pltpu.make_async_copy(a.at[part], b.at[part], suf_sem.at[i * chunks + c])
            )
    for c in halves:
        c.start()

    barrier = pltpu.get_barrier_semaphore()

    def greet(d, _):
        pl.semaphore_signal(
            barrier, inc=1, device_id={"sample": lax.rem(me + d, n)},
            device_id_type=pl.DeviceIdType.MESH,
        )
        return 0

    lax.fori_loop(1, n, greet, 0)

    for src, copy, dst, mine in ((pk, local[0], k_send, k_all), (pv, local[1], v_send, v_all)):
        copy.wait()
        wide[...] = src[...].astype(F32)
        for h in range(kvh):
            dst[h] = wide[pl.ds(h, tokens, stride=kvh), :].astype(BF16)
        mine[head] = wide[pl.ds(head, tokens, stride=kvh), :].astype(BF16)

    pl.semaphore_wait(barrier, n - 1)

    def q_copy(d):
        dev = lax.rem(me + d, n)
        return remote(q_hbm.at[:, lax.rem(dev, kvh)], q_all.at[me], q_ss.at[d], q_rs.at[me], dev)

    def kv_copy(d, src, dst, ss, rs):
        hd = lax.rem(head + d, kvh)
        return remote(src.at[hd], dst.at[head], ss.at[d], rs.at[head], base + hd)

    def start(copy):
        def body(d, _):
            copy(d).start()
            return 0
        return body

    k_copy = lambda d: kv_copy(d, k_send, k_all, k_ss, k_rs)
    v_copy = lambda d: kv_copy(d, v_send, v_all, v_ss, v_rs)
    lax.fori_loop(1, n, start(q_copy), 0)
    lax.fori_loop(1, kvh, start(k_copy), 0)
    lax.fori_loop(1, kvh, start(v_copy), 0)

    for c in local[2:]:
        c.wait()
    rows = kvh * per
    q_rows = jnp.concatenate(
        [q_own[t, h].astype(F32) for h in range(kvh) for t in range(steps)], axis=0
    ).astype(BF16)
    length = len_own[0]
    row = lax.broadcasted_iota(jnp.int32, (rows, 128), 0)
    lane = lax.broadcasted_iota(jnp.int32, (rows, 128), 1)
    lane_head = lax.rem(lane, kvh)
    match = (row >= lane_head * per) & (row < (lane_head + 1) * per)
    bias = jnp.where(match, 0.0, -jnp.inf).astype(F32)
    bias_wide = jnp.concatenate([bias] * (chunk // 128), axis=1)
    token_of = lax.div(lax.broadcasted_iota(jnp.int32, (8, chunk), 1), kvh)

    top = jnp.full((rows, 1), -jnp.inf, F32)
    for c in range(chunks):
        halves[c].wait()
        s = nt_dot(q_rows, sk[c * chunk:(c + 1) * chunk, :]) * factor
        limit = jnp.where(token_of < length - c * (chunk // kvh), 0.0, -jnp.inf).astype(F32)[:1]
        s = s + bias_wide + limit
        s_own[c] = s
        top = jnp.maximum(top, jnp.max(s, axis=-1, keepdims=True))

    pad = jnp.zeros((128 - steps * kvh, dim), F32)
    new_k = jnp.concatenate([nk[j].astype(F32) for j in range(steps)] + [pad], axis=0).astype(BF16)
    new_v = jnp.concatenate([nv[j].astype(F32) for j in range(steps)] + [pad], axis=0).astype(BF16)
    step_of = lax.div(lax.rem(row, per), gsize)
    s_new = nt_dot(q_rows, new_k) * factor + bias
    s_new = jnp.where(lax.div(lane, kvh) <= step_of, s_new, -jnp.inf)
    own_max = jnp.maximum(top, jnp.max(s_new, axis=-1, keepdims=True))
    w_new = jnp.exp(s_new - own_max)
    own_total = jnp.sum(w_new, axis=-1, keepdims=True)
    own_sum = jnp.dot(w_new.astype(BF16), new_v, preferred_element_type=F32)
    for c in range(chunks):
        halves[chunks + c].wait()
        w = jnp.exp(s_own[c] - own_max)
        own_total = own_total + jnp.sum(w, axis=-1, keepdims=True)
        own_sum = own_sum + jnp.dot(
            w.astype(BF16), sv[c * chunk:(c + 1) * chunk, :], preferred_element_type=F32
        )

    own_q.wait()

    def arrive(make, rs):
        def body(d, _):
            make(d, rs).wait_recv()
            return 0
        return body

    def q_in(d, _):
        src = lax.rem(me + d, n)
        return remote(q_hbm.at[:, head], q_all.at[src], q_ss.at[d], q_rs.at[src], src)

    def kv_in(src, dst, ss, rs):
        def make(d, _):
            hd = lax.rem(head + d, kvh)
            return remote(src.at[hd], dst.at[hd], ss.at[d], rs.at[hd], base + hd)
        return make

    lax.fori_loop(1, n, arrive(q_in, None), 0)
    lax.fori_loop(1, kvh, arrive(kv_in(k_send, k_all, k_ss, k_rs), None), 0)

    diag_row = lax.broadcasted_iota(jnp.int32, (per, 128), 0)
    diag_lane = lax.broadcasted_iota(jnp.int32, (per, 128), 1)
    diag = diag_row == diag_lane

    def out_copy(dev):
        return remote(o_send.at[dev], o_all.at[me], o_ss.at[dev], o_rs.at[me], dev)

    def log_copy(dev):
        return remote(l_send.at[dev], l_all.at[me], l_ss.at[dev], l_rs.at[me], dev)

    keys = k_all[...].reshape(kvh * tokens, dim)
    groups = n // group
    span = group * per

    def first_of(i):
        return lax.rem(base + kvh + i * group, n)

    def weigh(i, _):
        first = first_of(i)
        at = pl.ds(pl.multiple_of(first * per, span), span)
        q_block = rows_of(q_all[pl.ds(first, group)]).astype(BF16)
        s = nt_dot(q_block, keys) * factor
        m = jnp.max(s, axis=-1, keepdims=True)
        w = jnp.exp(s - m)
        total = jnp.sum(w, axis=-1, keepdims=True)
        high = w.astype(BF16)
        w_high[at] = high
        w_low[at] = (w - high.astype(F32)).astype(BF16)
        total_all[at] = total
        logs = jnp.broadcast_to(m + jnp.log(total), (span, 128)).reshape(group, per, 128)
        l_send[pl.ds(first, group)] = jnp.sum(
            jnp.where(diag[None], logs, 0.0), axis=1, keepdims=True
        )
        for j in range(group):
            dev = first + j

            @pl.when(dev != me)
            def _():
                log_copy(dev).start()

        return 0

    lax.fori_loop(0, groups, weigh, 0)
    lax.fori_loop(1, kvh, arrive(kv_in(v_send, v_all, v_ss, v_rs), None), 0)
    values = v_all[...].reshape(kvh * tokens, dim)

    def block(i, _):
        first = first_of(i)
        at = pl.ds(pl.multiple_of(first * per, span), span)
        sums = jnp.dot(w_high[at], values, preferred_element_type=F32) + jnp.dot(
            w_low[at], values, preferred_element_type=F32
        )
        o_send[pl.ds(first, group)] = (sums / total_all[at]).reshape(group, per, dim)
        for j in range(group):
            dev = first + j

            @pl.when(dev != me)
            def _():
                out_copy(dev).start()

        return 0

    lax.fori_loop(0, groups, block, 0)
    mine_o = pltpu.make_async_copy(o_send.at[me], o_all.at[me], o_rs.at[me])
    mine_l = pltpu.make_async_copy(l_send.at[me], l_all.at[me], l_rs.at[me])
    mine_o.start()
    mine_l.start()

    def drain(d, _):
        q_copy(d).wait_send()
        return 0

    def drain_kv(d, _):
        k_copy(d).wait_send()
        v_copy(d).wait_send()
        return 0

    lax.fori_loop(1, n, drain, 0)
    lax.fori_loop(1, kvh, drain_kv, 0)
    mine_o.wait()
    mine_l.wait()

    def results_in(d, _):
        src = lax.rem(me + d, n)
        remote(o_send.at[src], o_all.at[src], o_ss.at[src], o_rs.at[src], src).wait_recv()
        remote(l_send.at[src], l_all.at[src], l_ss.at[src], l_rs.at[src], src).wait_recv()
        return 0

    lax.fori_loop(1, n, results_in, 0)

    repeats = n // kvh
    logs = jnp.sum(
        jnp.where(diag[None], jnp.broadcast_to(l_all[...], (n, per, 128)), 0.0),
        axis=-1, keepdims=True,
    ).reshape(repeats, rows, 1)
    largest = jnp.maximum(jnp.max(logs, axis=0), own_max)
    weights = jnp.exp(logs - largest[None])
    share = jnp.exp(own_max - largest)
    upper = share * own_sum
    lower = share * own_total
    for r in range(repeats):
        piece = o_all[r * kvh:(r + 1) * kvh].reshape(rows, dim)
        upper = upper + weights[r] * piece
        lower = lower + weights[r]
    result = upper / lower
    for h in range(kvh):
        for t in range(steps):
            at = h * per + t * gsize
            out_ref[t, h] = result[at:at + gsize]

    def drain_out(d, _):
        dev = lax.rem(me + d, n)
        out_copy(dev).wait_send()
        log_copy(dev).wait_send()
        return 0

    lax.fori_loop(1, n, drain_out, 0)


def solution(mesh):
    n = mesh.shape["sample"]

    def shards(queries, pk, pv, sk, sv, lengths, nk, nv):
        _, steps, heads, dim = queries.shape
        tokens, kvh, _ = pk.shape
        gsize = heads // kvh
        suffix = sk.shape[1]
        per = steps * gsize
        group = math.gcd(n, 4)
        chunk = math.gcd(suffix * kvh, 1024)
        chunks = suffix * kvh // chunk
        any_spec = pl.BlockSpec(memory_space=pl.ANY)
        dma = pltpu.SemaphoreType.DMA
        out = pl.pallas_call(
            functools.partial(kernel, n, group, chunk),
            out_shape=jax.ShapeDtypeStruct((steps, kvh, gsize, dim), F32),
            in_specs=[any_spec] + [pl.BlockSpec(memory_space=pltpu.HBM)] * 7,
            out_specs=pl.BlockSpec(memory_space=pltpu.VMEM),
            scratch_shapes=[
                pltpu.VMEM((steps, kvh, gsize, dim), BF16),
                pltpu.VMEM((tokens * kvh, dim), BF16),
                pltpu.VMEM((tokens * kvh, dim), BF16),
                pltpu.VMEM((tokens * kvh, dim), F32),
                pltpu.VMEM((kvh, tokens, dim), BF16),
                pltpu.VMEM((kvh, tokens, dim), BF16),
                pltpu.VMEM((n, steps, gsize, dim), BF16),
                pltpu.VMEM((kvh, tokens, dim), BF16),
                pltpu.VMEM((kvh, tokens, dim), BF16),
                pltpu.VMEM((suffix * kvh, dim), BF16),
                pltpu.VMEM((suffix * kvh, dim), BF16),
                pltpu.VMEM((steps, kvh, dim), BF16),
                pltpu.VMEM((steps, kvh, dim), BF16),
                pltpu.VMEM((chunks, kvh * per, chunk), F32),
                pltpu.VMEM((n, per, dim), F32),
                pltpu.VMEM((n, 1, 128), F32),
                pltpu.VMEM((n, per, dim), F32),
                pltpu.VMEM((n, 1, 128), F32),
                pltpu.SMEM((1,), jnp.int32),
                pltpu.VMEM((n * per, kvh * tokens), BF16),
                pltpu.VMEM((n * per, kvh * tokens), BF16),
                pltpu.VMEM((n * per, 1), F32),
                dma((6,)), dma((2 * chunks,)),
                dma((n,)), dma((n,)), dma((kvh,)), dma((kvh,)), dma((kvh,)), dma((kvh,)),
                dma((n,)), dma((n,)), dma((n,)), dma((n,)),
            ],
            compiler_params=pltpu.CompilerParams(
                collective_id=0, has_side_effects=True, vmem_limit_bytes=48 << 20
            ),
        )(lengths, *[pltpu.with_memory_space_constraint(x, pltpu.HBM) for x in (
            queries.reshape(steps, kvh, gsize, dim),
            pk.reshape(tokens * kvh, dim),
            pv.reshape(tokens * kvh, dim),
            sk.reshape(suffix * kvh, dim),
            sv.reshape(suffix * kvh, dim),
            nk.reshape(steps, kvh, dim),
            nv.reshape(steps, kvh, dim),
        )])
        return out.reshape(1, steps, heads, dim)

    spread = ("group", "sample")
    four = P(spread, None, None, None)
    three = P(spread, None, None)
    return jax.shard_map(
        shards, mesh=mesh,
        in_specs=(four, three, three, four, four, P(spread), four, four),
        out_specs=four, check_vma=False,
    )
```
